256 devices in a mesh: cluster: 32 (over z, y), group: 8 (over x, core).
Axes of the slice: x: 4, y: 4, z: 8, core: 2. Of those that a mesh axis runs over, the one named last changes fastest.
Arguments:
- loads: bfloat16 [512, 131072], P('group', 'cluster'), may hold values from -6 to 6
- near_blocks: bfloat16 [512, 24, 256, 256], P('cluster', 'group'), may hold values from -0.078125 to 0.078125
- near_cols: int32 [512, 24], P('cluster'), may hold values from 0 to 511, as said below
- far_right: bfloat16 [512, 64, 256], P('cluster'), may hold values from -0.375 to 0.375
- far_coupling: bfloat16 [512, 64, 1024], P('cluster'), may hold values from -0.1875 to 0.1875
- far_left: bfloat16 [512, 64, 256], P('cluster'), may hold values from -0.75 to 0.75
- far_cols: int32 [512, 16], P('cluster'), may hold values from 0 to 511, as said below
Outputs:
- response: bfloat16 [512, 131072], P('group', 'cluster')
The draws below stay inside these ranges and needn't reach their ends.
Inputs may be any that keep to these rules, and one draw needn't show every extreme that they name: `near_cols`: the 24 entries of a row are distinct leaves i + d modulo 512, with |d| <= 16, for row leaf i. `far_cols`: the 16 entries of a row are distinct leaves i + d modulo 512, with 16 < d < 496, for row leaf i.
All inputs are finite; a program needn't handle non-finite values.
Results may differ from the reference program's by a relative error of at most 0.0049.
Values may be sent and summed in bfloat16 or wider, within the bound.
No kernel may reach another device: no remote copies, remote signals or barrier semaphores. Data moves between devices by JAX's collectives and lax.ppermute only.
A program may use at most 128 MiB of HBM per device.

```python
import jax
import jax.numpy as jnp
from jax import lax

LEAF = 256
RANK = 64
LOADS = 512
NNEAR = 24
REACH = 16
NFAR = 16
NL = 512
PANELS = 131072


def draw_near_cols(key, part):
    span = 2 * REACH + 1
    scores = jax.random.randint(key, (NL, span), 0, 1 << 16) * span + jnp.arange(span, dtype=jnp.int32)[None, :]
    order = jnp.argsort(scores, axis=1, stable=True)[:, :NNEAR].astype(jnp.int32)
    return (jnp.arange(NL, dtype=jnp.int32)[:, None] + order - REACH) % NL


def draw_far_cols(key, part):
    span = NL - 2 * REACH - 1
    scores = jax.random.randint(key, (NL, span), 0, 1 << 16) * span + jnp.arange(span, dtype=jnp.int32)[None, :]
    order = jnp.argsort(scores, axis=1, stable=True)[:, :NFAR].astype(jnp.int32)
    return (jnp.arange(NL, dtype=jnp.int32)[:, None] + order + REACH + 1) % NL


def block_scale(rng, extent, cuts, smallest, top_value):
    def one(axis_at, blocks):
        steps = jax.random.uniform(jax.random.fold_in(jax.random.fold_in(rng, 6), axis_at), (blocks,), jnp.float32, smallest / len(cuts), top_value / len(cuts))
        return jnp.repeat(jnp.exp(steps), extent[axis_at] // blocks).reshape((-1,) + (1,) * (len(extent) - axis_at - 1))

    factor_of = one(*cuts[0])
    for cut in cuts[1:]:
        factor_of = factor_of * one(*cut)
    return factor_of


def gaussian(stream_key, shape, width, bound, shards=(), kind=jnp.bfloat16):
    entries = width * jax.random.normal(stream_key, shape, jnp.float32)
    if shards:
        entries = entries * block_scale(stream_key, shape, shards, -0.22, 0.18)
    return jnp.clip(entries, -bound, bound).astype(kind)


def setup_inputs(seed: int = 0) -> dict:
    streams_of = jax.random.split(jax.random.key(seed), 8)
    loads = gaussian(streams_of[0], (LOADS, PANELS), 1.0, 6.0, ((0, 8), (1, 32)))
    near_blocks = gaussian(streams_of[1], (NL, NNEAR, LEAF, LEAF), (LEAF * NNEAR) ** -0.5, 0.078125, ((0, 32), (1, 8)))
    near_cols = draw_near_cols(jax.random.fold_in(streams_of[7], 71), 0)
    far_right = gaussian(streams_of[3], (NL, RANK, LEAF), LEAF ** -0.5, 0.375, ((0, 32),))
    far_coupling = gaussian(streams_of[4], (NL, RANK, NFAR * RANK), (RANK * NFAR) ** -0.5, 0.1875, ((0, 32),))
    far_left = gaussian(streams_of[5], (NL, RANK, LEAF), RANK ** -0.5, 0.75, ((0, 32),))
    far_cols = draw_far_cols(jax.random.fold_in(streams_of[7], 71), 0)
    return {"loads": loads, "near_blocks": near_blocks, "near_cols": near_cols, "far_right": far_right, "far_coupling": far_coupling, "far_left": far_left, "far_cols": far_cols}


def reference(loads, near_blocks, near_cols, far_right, far_coupling, far_left, far_cols):
    patterns = loads.shape[0]
    leaves = near_blocks.shape[0]
    rank = far_right.shape[1]
    per_leaf = loads.reshape(patterns, leaves, LEAF)
    coef = jnp.einsum('rlc,lac->lra', per_leaf.astype(jnp.float32), far_right.astype(jnp.float32)).astype(jnp.bfloat16)

    def one_leaf(index):
        picked = jnp.take(per_leaf, near_cols[index], axis=1).astype(jnp.float32)
        near = jnp.einsum('rkc,knc->rn', picked, near_blocks[index].astype(jnp.float32))
        chosen = jnp.take(coef, far_cols[index], axis=0).astype(jnp.float32)
        coupling = far_coupling[index].reshape(rank, NFAR, rank).astype(jnp.float32)
        reduced = jnp.einsum('kra,akb->rb', chosen, coupling).astype(jnp.bfloat16)
        far = jnp.dot(reduced, far_left[index], preferred_element_type=jnp.float32)
        return (near + far).astype(jnp.bfloat16)

    blocks = lax.map(one_leaf, jnp.arange(leaves, dtype=jnp.int32))
    return jnp.transpose(blocks, (1, 0, 2)).reshape(patterns, leaves * LEAF)
```

```python
import functools

import jax
import jax.numpy as jnp
from jax import lax
from jax.experimental import pallas as pl
from jax.experimental.pallas import tpu as pltpu
from jax.sharding import Mesh, PartitionSpec as P


NX, NY, NZ, NCORE = 4, 4, 8, 2
CLUSTER = ("z", "y")
GROUP = ("x", "core")


def shift(size, step):
    return [(i, (i - step) % size) for i in range(size)]


def nt(a, b):
    return lax.dot_general(a, b, (((1,), (1,)), ((), ())), preferred_element_type=jnp.float32)


def coef_kernel(x_ref, right_ref, out_ref):
    leaves, rank, leaf = right_ref.shape
    for l in range(leaves):
        value = nt(x_ref[:, l * leaf : (l + 1) * leaf], right_ref[l])
        out_ref[:, l * rank : (l + 1) * rank] = value.astype(jnp.bfloat16)


def coefficients(loads, far_right):
    leaves, rank, leaf = far_right.shape
    return pl.pallas_call(
        coef_kernel,
        out_shape=jax.ShapeDtypeStruct((loads.shape[0], leaves * rank), jnp.bfloat16),
        cost_estimate=pl.CostEstimate(
            flops=2 * loads.shape[0] * leaves * rank * leaf, bytes_accessed=1 << 20, transcendentals=0
        ),
        name="coef",
    )(loads, far_right)


def near_kernel(per_step, shards, reach, cols_ref, mine_ref, other_ref, *rest):
    sources = rest[: 3 * shards]
    outs = rest[3 * shards : 4 * shards]
    window, sem = rest[4 * shards :]
    rows, width = sources[0].shape
    leaf = mine_ref.shape[-1]
    per_group = mine_ref.shape[1]
    step = pl.program_id(0)
    leaves = width // leaf
    spread = 3 * leaves
    total = NZ * NY * leaves

    def copies():
        return [
            pltpu.make_async_copy(
                sources[3 * s + seg],
                window.at[pl.ds(s * rows, rows), pl.ds(seg * width, width)],
                sem.at[3 * s + seg],
            )
            for s in range(shards)
            for seg in range(3)
        ]

    @pl.when(step == 0)
    def _():
        for c in copies():
            c.start()
        for c in copies():
            c.wait()

    cluster = lax.axis_index("z") * NY + lax.axis_index("y")
    core = lax.axis_index("core")
    group = lax.axis_index("x") * NCORE
    first = cluster * leaves - reach
    for q in range(per_step):
        m = step * per_step + q
        acc = None
        for blocks, owner in ((mine_ref, group + core), (other_ref, group + 1 - core)):
            for k in range(per_group):
                col = cols_ref[m, owner * per_group + k]
                at = lax.rem(col - first + 2 * total, total)
                at = jnp.minimum(at, spread - 1)
                picked = window[:, pl.ds(pl.multiple_of(at * leaf, leaf), leaf)]
                value = nt(picked, blocks[q, k])
                acc = value if acc is None else acc + value
        for s in range(shards):
            outs[s][:, q * leaf : (q + 1) * leaf] = acc[s * rows : (s + 1) * rows].astype(outs[s].dtype)


def near_field(near_cols, mine, other, sources, dtypes, reach=16, per_step=2):
    shards = len(dtypes)
    leaves, per_group, leaf, _ = mine.shape
    rows, width = sources[0].shape
    blocks = pl.BlockSpec((per_step, per_group, leaf, leaf), lambda i, cols: (i, 0, 0, 0))
    return pl.pallas_call(
        functools.partial(near_kernel, per_step, shards, reach),
        grid_spec=pltpu.PrefetchScalarGridSpec(
            num_scalar_prefetch=1,
            grid=(leaves // per_step,),
            in_specs=[blocks, blocks] + [pl.BlockSpec(memory_space=pl.ANY)] * (3 * shards),
            out_specs=[pl.BlockSpec((rows, per_step * leaf), lambda i, cols: (0, i))] * shards,
            scratch_shapes=[
                pltpu.VMEM((shards * rows, 3 * width), jnp.bfloat16),
                pltpu.SemaphoreType.DMA((3 * shards,)),
            ],
        ),
        out_shape=[jax.ShapeDtypeStruct((rows, width), t) for t in dtypes],
        compiler_params=pltpu.CompilerParams(dimension_semantics=("arbitrary",), vmem_limit_bytes=32 << 20),
        cost_estimate=pl.CostEstimate(
            flops=2 * shards * rows * leaves * 2 * per_group * leaf * leaf,
            bytes_accessed=4 * leaves * per_group * leaf * leaf + 2 * shards * rows * width * 4,
            transcendentals=0,
        ),
        name="near",
    )(near_cols, mine, other, *sources)


def far_kernel(per_step, cols_ref, coupling_ref, left_ref, *rest):
    parts = rest[:NZ]
    out_ref, table, sem = rest[NZ:]
    slots, rows, width = parts[0].shape
    rank = coupling_ref.shape[1]
    count = coupling_ref.shape[2] // rank
    leaf = left_ref.shape[2]
    leaves = width // rank
    step = pl.program_id(0)

    def copies():
        return [
            pltpu.make_async_copy(
                parts[s].at[t],
                table.at[:, pl.ds((s * slots + t) * width, width)],
                sem.at[s * slots + t],
            )
            for s in range(NZ)
            for t in range(slots)
        ]

    @pl.when(step == 0)
    def _():
        for c in copies():
            c.start()
        for c in copies():
            c.wait()

    z, y = lax.axis_index("z"), lax.axis_index("y")
    half = lax.broadcasted_iota(jnp.int32, (rows, 2 * rank), 1) // rank
    for q in range(per_step):
        chosen = []
        for k in range(count):
            col = cols_ref[step * per_step + q, k]
            owner = col // leaves
            dz = lax.rem(owner // NY - z + NZ, NZ)
            dy = lax.rem(lax.rem(owner, NY) - y + NY, NY)
            slot = dz * NY + dy
            at = slot * width + (lax.rem(col, leaves) // 2) * (2 * rank)
            pair = table[:, pl.ds(pl.multiple_of(at, 2 * rank), 2 * rank)]
            chosen.append(jnp.where(half == lax.rem(col, 2), pair, jnp.zeros_like(pair)))
        even = jnp.concatenate(chosen[0::2], axis=1)
        odd = jnp.concatenate(chosen[1::2], axis=1)
        pieces = [coupling_ref[q, :, p * 2 * rank : (p + 1) * 2 * rank] for p in range(count // 2)]
        stacked = jnp.concatenate([piece for piece in pieces for _ in range(2)], axis=0)
        both = jnp.dot(jnp.concatenate([even, odd], axis=0), stacked, preferred_element_type=jnp.float32)
        z_value = both[:rows, :rank] + both[rows:, rank:]
        out_ref[:, q * leaf : (q + 1) * leaf] = jnp.dot(
            z_value.astype(jnp.bfloat16), left_ref[q], preferred_element_type=jnp.float32
        )


def far_field(far_cols, coupling, left, parts, per_step=4):
    leaves, rank, wide = coupling.shape
    leaf = left.shape[2]
    slots, rows, width = parts[0].shape
    return pl.pallas_call(
        functools.partial(far_kernel, per_step),
        grid_spec=pltpu.PrefetchScalarGridSpec(
            num_scalar_prefetch=1,
            grid=(leaves // per_step,),
            in_specs=[
                pl.BlockSpec((per_step, rank, wide), lambda i, cols: (i, 0, 0)),
                pl.BlockSpec((per_step, rank, leaf), lambda i, cols: (i, 0, 0)),
            ]
            + [pl.BlockSpec(memory_space=pl.ANY)] * NZ,
            out_specs=pl.BlockSpec((rows, per_step * leaf), lambda i, cols: (0, i)),
            scratch_shapes=[
                pltpu.VMEM((rows, NZ * slots * width), jnp.bfloat16),
                pltpu.SemaphoreType.DMA((NZ * slots,)),
            ],
        ),
        out_shape=jax.ShapeDtypeStruct((rows, leaves * leaf), jnp.float32),
        compiler_params=pltpu.CompilerParams(dimension_semantics=("arbitrary",), vmem_limit_bytes=32 << 20),
        cost_estimate=pl.CostEstimate(
            flops=2 * leaves * rows * (2 * wide * 2 * rank + rank * leaf),
            bytes_accessed=9 << 20,
            transcendentals=0,
        ),
        name="far",
    )(far_cols, coupling, left, *parts)


def local(loads, near_blocks, near_cols, far_right, far_coupling, far_left, far_cols):
    other = lax.ppermute(near_blocks, "core", shift(NCORE, 1))
    from_cluster = lambda a, step: lax.ppermute(a, CLUSTER, shift(NZ * NY, step))
    from_x = lambda a, step: lax.ppermute(a, "x", shift(NX, step))

    coef = coefficients(loads, far_right)
    left, right = from_cluster(loads, -1), from_cluster(loads, 1)
    own = [loads, from_x(loads, 1), from_x(loads, 2), from_x(loads, 3)]
    row = jnp.stack([coef] + [lax.ppermute(coef, "y", shift(NY, t)) for t in range(1, NY)])
    parts = [row] + [None] * (NZ - 1)
    ahead = behind = row
    for s in range(1, NZ // 2 + 1):
        ahead = lax.ppermute(ahead, "z", shift(NZ, 1))
        parts[s] = ahead
        if s < NZ // 2:
            behind = lax.ppermute(behind, "z", shift(NZ, -1))
            parts[NZ - s] = behind

    lefts = [left, from_x(left, 1), from_cluster(own[2], -1), from_x(left, 3)]
    rights = [right, from_x(right, 1), from_cluster(own[2], 1), from_x(right, 3)]
    sources = [a for s in range(NX) for a in (lefts[s], own[s], rights[s])]
    partial = near_field(
        near_cols, near_blocks, other, sources, [jnp.float32, jnp.bfloat16, jnp.bfloat16, jnp.bfloat16]
    )
    far = far_field(far_cols, far_coupling, far_left, parts)
    near = partial[0]
    for s in range(1, NX):
        near = near + lax.ppermute(partial[s], "x", shift(NX, -s)).astype(jnp.float32)
    return (near + far).astype(jnp.bfloat16)


def solution(mesh):
    fine = Mesh(mesh.devices.reshape(NZ, NY, NX, NCORE), CLUSTER + GROUP)
    placed = (
        P(GROUP, CLUSTER),
        P(CLUSTER, GROUP, None, None),
        P(CLUSTER, None),
        P(CLUSTER, None, None),
        P(CLUSTER, None, None),
        P(CLUSTER, None, None),
        P(CLUSTER, None),
    )
    return jax.shard_map(local, mesh=fine, in_specs=placed, out_specs=P(GROUP, CLUSTER), check_vma=False)
```
